32 devices in a mesh: row: 4 (over y, x), col: 8 (over z, core).
Axes of the slice: x: 2, y: 2, z: 4, core: 2. Of those that a mesh axis runs over, the one named last changes fastest.
Arguments:
- points: bfloat16 [8192, 256], P(('row', 'col')), may hold values from -0.4 to 0.4, as said below
- spread: float32 [8192], P(('row', 'col')), may hold values from 1 to 12
- vectors: bfloat16 [8192, 64], P(('row', 'col')), may hold values from -6 to 6
Outputs:
- product: float32 [8192, 64], P(('row', 'col'))
The draws below stay inside these ranges and needn't reach their ends.
Inputs may be any that keep to these rules, and one draw needn't show every extreme that they name: `points`: embedding entries are real values of order 0.1.
All inputs are finite; a program needn't handle non-finite values.
Results may differ from the reference program's by a relative error of at most 0.0085.
Values may be sent and summed in bfloat16 or wider, within the bound.
A program may use at most 128 MiB of HBM per device.

```python
import math
import jax
import jax.numpy as jnp
from jax import lax

F = 256
K = 64
NPTS = 8192


def draw_points(key, part):
    first_key = jax.random.fold_in(jax.random.fold_in(key, 17), 0)
    base = jnp.clip(jax.random.normal(first_key, (NPTS, F), jnp.float32), -6.0, 6.0)
    return (base * 0.0625).astype(jnp.bfloat16)


def levels(key, extent, shards, least, largest):
    loudness, own = 1.0, jax.random.fold_in(key, 6)
    for dim, shards_of in shards:
        steps = jnp.exp(jax.random.uniform(jax.random.fold_in(own, dim), (shards_of,), jnp.float32, least / len(shards), largest / len(shards)))
        loudness = loudness * jnp.repeat(steps, extent[dim] // shards_of).reshape([-1 if axis == dim else 1 for axis in range(len(extent))])
    return loudness


def scatter_about(stream_key, extent, width, reach, cuts=(), kind=jnp.bfloat16):
    values = width * jax.random.normal(stream_key, extent, jnp.float32)
    if cuts:
        values = values * levels(stream_key, extent, cuts, -0.22, 0.18)
    return jnp.clip(values, -reach, reach).astype(kind)


def setup_inputs(seed: int = 0) -> dict:
    arg_keys = jax.random.split(jax.random.key(seed), 4)
    points = draw_points(jax.random.fold_in(arg_keys[3], 71), 0)
    spread = jnp.clip(jnp.exp(math.log(12.0) - 2.4849066 * jax.random.uniform(arg_keys[1], (NPTS,), jnp.float32) ** levels(arg_keys[1], (NPTS,), ((0, 32),), -0.2, 0.2)), 1.0, 12.0)
    vectors = scatter_about(arg_keys[2], (NPTS, K), 1.0, 6.0, ((0, 32),))
    return {"points": points, "spread": spread, "vectors": vectors}


def reference(points, spread, vectors):
    total_rows = points.shape[0]
    block_rows = min(1024, total_rows)
    count = total_rows // block_rows
    point_f = points.astype(jnp.float32)
    squares = jnp.sum(point_f * point_f, axis=1)
    col_ids = jnp.arange(total_rows, dtype=jnp.int32)
    vec_f = vectors.astype(jnp.float32)

    def one_block(carry, index):
        start = (index * block_rows).astype(jnp.int32)
        rows = lax.dynamic_slice_in_dim(points, start, block_rows, 0)
        row_sq = lax.dynamic_slice_in_dim(squares, start, block_rows, 0)
        row_bw = lax.dynamic_slice_in_dim(spread, start, block_rows, 0)
        row_vec = lax.dynamic_slice_in_dim(vec_f, start, block_rows, 0)
        cross = jnp.dot(rows, points.T, preferred_element_type=jnp.float32)
        dist = row_sq[:, None] + squares[None, :] - 2.0 * cross
        row_ids = start + jnp.arange(block_rows, dtype=jnp.int32)
        kernel = jnp.where(row_ids[:, None] == col_ids[None, :], jnp.float32(0.0), jnp.exp(-row_bw[:, None] * dist))
        total = jnp.sum(kernel, axis=1)
        norm = (kernel / total[:, None]).astype(jnp.bfloat16)
        norm_f = norm.astype(jnp.float32)
        forward = jnp.dot(norm, vectors, preferred_element_type=jnp.float32)
        carry = carry + jnp.dot(norm_f.T, row_vec, preferred_element_type=jnp.float32)
        return carry, forward

    start_carry = jnp.zeros((total_rows, vectors.shape[1]), jnp.float32)
    backward, forwards = lax.scan(one_block, start_carry, jnp.arange(count, dtype=jnp.int32))
    forward = forwards.reshape(total_rows, vectors.shape[1])
    return 0.5 * (forward + backward)
```

```python
import functools
import math

import jax
import jax.numpy as jnp
from jax import lax
from jax.experimental import pallas as pl
from jax.experimental.pallas import tpu as pltpu
from jax.sharding import PartitionSpec as P

MESH = pl.DeviceIdType.MESH
LOG2E = math.log2(math.e)
VMEM_SPEC = pl.BlockSpec(memory_space=pltpu.VMEM)


def fold(block):
    half = block.shape[0] // 2
    return jnp.concatenate([block[:half], block[half:]], axis=1)


def unfold(block):
    width = block.shape[1] // 2
    return jnp.concatenate([block[:, :width], block[:, width:]], axis=0)


def kernel(
    n_rows, n_cols, pts_ref, bw_ref, vec_ref, out_ref,
    blk_pts, blk_vec, blk_aux, crs_pts, crs_aux, crs_col,
    fwd_acc, mirror, part, t_in, fwd_out, fwd_in, rev_out, rev_in,
    pts_s, pts_r, vec_s, vec_r, aux_s, aux_r,
    cp_s, cp_r, ca_s, ca_r, t_s, t_r, f_s, f_r, g_s, g_r,
):
    row = lax.axis_index("row")
    col = lax.axis_index("col")
    share = pts_ref.shape[0]

    def col_peer(x):
        return {"col": lax.bitwise_xor(col, x)}

    def row_peer(x):
        return {"row": lax.bitwise_xor(row, x)}

    barrier = pltpu.get_barrier_semaphore()
    for x in range(1, n_cols):
        pl.semaphore_signal(barrier, inc=1, device_id=col_peer(x), device_id_type=MESH)
    for x in range(1, n_rows):
        pl.semaphore_signal(barrier, inc=1, device_id=row_peer(x), device_id_type=MESH)

    blk_pts[0] = pts_ref[...]
    blk_vec[0] = fold(vec_ref[...])
    pl.semaphore_wait(barrier, n_cols + n_rows - 2)

    def send(buf, src, dst, send_sem, recv_sem, peer):
        copy = pltpu.make_async_remote_copy(
            src_ref=buf.at[src], dst_ref=buf.at[dst], send_sem=send_sem.at[dst],
            recv_sem=recv_sem.at[dst], device_id=peer, device_id_type=MESH,
        )
        copy.start()
        return copy

    pts, vec, aux, cpts, caux = {}, {}, {}, {}, {}
    near = list(range(2, n_cols, 2))
    for x in near:
        pts[x] = send(blk_pts, 0, x, pts_s, pts_r, col_peer(x))
    for x in range(1, n_rows):
        copy = pltpu.make_async_remote_copy(
            src_ref=blk_pts.at[0], dst_ref=crs_pts.at[x], send_sem=cp_s.at[x],
            recv_sem=cp_r.at[x], device_id=row_peer(x), device_id_type=MESH,
        )
        copy.start()
        cpts[x] = copy
    for x in near:
        vec[x] = send(blk_vec, 0, x, vec_s, vec_r, col_peer(x))
    pts[1] = send(blk_pts, 0, 1, pts_s, pts_r, col_peer(1))
    vec[1] = send(blk_vec, 0, 1, vec_s, vec_r, col_peer(1))

    own = pts_ref[...].astype(jnp.float32)
    half_sq = 0.5 * jnp.sum(own * own, axis=1, keepdims=True)
    wide = jnp.transpose(jnp.broadcast_to(half_sq, (share, 128)))
    my_aux = jnp.concatenate([bw_ref[...] * (2.0 * LOG2E), wide[0:1]], axis=0)
    blk_aux[0] = my_aux
    crs_aux[0] = my_aux
    for x in near + [1]:
        aux[x] = send(blk_aux, 0, x, aux_s, aux_r, col_peer(x))
    for x in range(1, n_rows):
        caux[x] = send(crs_aux, 0, x, ca_s, ca_r, row_peer(x))
    crs_pts[0] = pts_ref[...]

    def column(m):
        rows = crs_aux[m]
        padded = jnp.concatenate([rows, jnp.zeros((6, share), jnp.float32)], axis=0)
        crs_col[m] = jnp.transpose(padded)

    def tile(m, b, vb, arow, hrow, diagonal):
        cols = crs_col[m]
        cross = lax.dot_general(
            crs_pts[m], blk_pts[b], (((1,), (1,)), ((), ())), preferred_element_type=jnp.float32
        )
        near_ = (cross - cols[:, 1:2]) - hrow
        first = jnp.exp2(near_ * cols[:, 0:1])
        second = jnp.exp2(near_ * arow)
        if diagonal:
            same = lax.broadcasted_iota(jnp.int32, (share, share), 0) == lax.broadcasted_iota(
                jnp.int32, (share, share), 1
            )
            first = jnp.where(same, 0.0, first)
            second = jnp.where(same, 0.0, second)
        product = jnp.dot(first.astype(jnp.bfloat16), vb, preferred_element_type=jnp.float32)
        if b == 0:
            fwd_acc[m] = product
        else:
            fwd_acc[m] += product
        mirror[m, :, b * share : (b + 1) * share] = second.astype(jnp.bfloat16)
        return jnp.sum(second, axis=0, keepdims=True)

    def step(b):
        vb = unfold(blk_vec[b])
        arow = blk_aux[b, 0:1]
        hrow = blk_aux[b, 1:2]
        if b == 0:
            column(0)
            total = tile(0, 0, vb, arow, hrow, True)
            for m in range(1, n_rows):
                cpts[m].wait_recv()
                caux[m].wait_recv()
                column(m)
                total = total + tile(m, 0, vb, arow, hrow, False)
        else:
            total = lax.fori_loop(
                0, n_rows,
                lambda m, acc: acc + tile(m, b, vb, arow, hrow, False),
                jnp.zeros((1, share), jnp.float32),
            )
        part[b : b + 1] = total

    step(0)
    for b in range(1, n_cols):
        if b % 2 == 1 and b > 1:
            pass
        pts[b].wait_recv()
        vec[b].wait_recv()
        aux[b].wait_recv()
        if b % 2 == 0:
            pts[b + 1] = send(blk_pts, b, b + 1, pts_s, pts_r, col_peer(1))
            vec[b + 1] = send(blk_vec, b, b + 1, vec_s, vec_r, col_peer(1))
            aux[b + 1] = send(blk_aux, b, b + 1, aux_s, aux_r, col_peer(1))
        step(b)

    totals = {}
    for x in range(1, n_cols):
        copy = pltpu.make_async_remote_copy(
            src_ref=part, dst_ref=t_in.at[x], send_sem=t_s.at[x], recv_sem=t_r.at[x],
            device_id=col_peer(x), device_id_type=MESH,
        )
        copy.start()
        totals[x] = copy
    fwd, rev = {}, {}
    for m in range(1, n_rows):
        fwd_out[m] = fold(fwd_acc[m]).astype(jnp.bfloat16)
        copy = pltpu.make_async_remote_copy(
            src_ref=fwd_out.at[m], dst_ref=fwd_in.at[m], send_sem=f_s.at[m], recv_sem=f_r.at[m],
            device_id=row_peer(m), device_id_type=MESH,
        )
        copy.start()
        fwd[m] = copy

    sums = [part[b : b + 1] for b in range(n_cols)]
    for x in range(1, n_cols):
        totals[x].wait_recv()
        other = t_in[x]
        for b in range(n_cols):
            sums[b] = sums[b] + other[x ^ b : (x ^ b) + 1]
    inverse = jnp.transpose(0.125 / jnp.concatenate(sums, axis=0))
    scaled = jnp.concatenate(
        [
            (unfold(blk_vec[b]).astype(jnp.float32) * inverse[:, b : b + 1]).astype(jnp.bfloat16)
            for b in range(n_cols)
        ],
        axis=0,
    )
    for m in range(1, n_rows):
        product = jnp.dot(mirror[m], scaled, preferred_element_type=jnp.float32)
        rev_out[m] = fold(product).astype(jnp.bfloat16)
        copy = pltpu.make_async_remote_copy(
            src_ref=rev_out.at[m], dst_ref=rev_in.at[m], send_sem=g_s.at[m], recv_sem=g_r.at[m],
            device_id=row_peer(m), device_id_type=MESH,
        )
        copy.start()
        rev[m] = copy
    reverse = jnp.dot(mirror[0], scaled, preferred_element_type=jnp.float32)
    forward = fwd_acc[0]
    for m in range(1, n_rows):
        fwd[m].wait_recv()
        forward = forward + unfold(fwd_in[m].astype(jnp.float32))
    for m in range(1, n_rows):
        rev[m].wait_recv()
        reverse = reverse + unfold(rev_in[m].astype(jnp.float32))
    out_ref[...] = 4.0 * (forward * inverse[:, 0:1] + reverse)
    for group in (pts, vec, aux, cpts, caux, totals, fwd, rev):
        for copy in group.values():
            copy.wait_send()


def local(n_rows, n_cols, points, spread, vectors):
    share, width = points.shape
    k = vectors.shape[1]
    f32, bf16 = jnp.float32, jnp.bfloat16
    dma = pltpu.SemaphoreType.DMA
    scratch = [
        pltpu.VMEM((n_cols, share, width), bf16),
        pltpu.VMEM((n_cols, share // 2, 2 * k), bf16),
        pltpu.VMEM((n_cols, 2, share), f32),
        pltpu.VMEM((n_rows, share, width), bf16),
        pltpu.VMEM((n_rows, 2, share), f32),
        pltpu.VMEM((n_rows, share, 8), f32),
        pltpu.VMEM((n_rows, share, k), f32),
        pltpu.VMEM((n_rows, share, n_cols * share), bf16),
        pltpu.VMEM((n_cols, share), f32),
        pltpu.VMEM((n_cols, n_cols, share), f32),
    ] + [pltpu.VMEM((n_rows, share // 2, 2 * k), bf16)] * 4
    scratch += [dma((n_cols,))] * 6 + [dma((n_rows,))] * 4 + [dma((n_cols,))] * 2
    scratch += [dma((n_rows,))] * 4
    return pl.pallas_call(
        functools.partial(kernel, n_rows, n_cols),
        out_shape=jax.ShapeDtypeStruct((share, k), f32),
        in_specs=[VMEM_SPEC] * 3,
        out_specs=VMEM_SPEC,
        scratch_shapes=scratch,
        compiler_params=pltpu.CompilerParams(
            collective_id=0, has_side_effects=True, vmem_limit_bytes=56 * 1024 * 1024
        ),
    )(points, spread.reshape(1, share), vectors)


def solution(mesh):
    placed = (P(("row", "col"), None), P(("row", "col")), P(("row", "col"), None))
    return jax.shard_map(
        functools.partial(local, mesh.shape["row"], mesh.shape["col"]),
        mesh=mesh, in_specs=placed, out_specs=P(("row", "col"), None), check_vma=False,
    )
```

```python
import functools
import math

import jax
import jax.numpy as jnp
from jax import lax
from jax.experimental import pallas as pl
from jax.experimental.pallas import tpu as pltpu
from jax.sharding import PartitionSpec as P

MESH = pl.DeviceIdType.MESH
LOG2E = math.log2(math.e)
VMEM_SPEC = pl.BlockSpec(memory_space=pltpu.VMEM)
HEAD = 16
NT = (((1,), (1,)), ((), ()))


def terms(value):
    high = value.astype(jnp.bfloat16)
    rest = value - high.astype(jnp.float32)
    middle = rest.astype(jnp.bfloat16)
    return [high, middle, (rest - middle.astype(jnp.float32)).astype(jnp.bfloat16)]


def untangle(head):
    head = head.astype(jnp.float32)
    return head[0:1] + head[1:2] + head[2:3], head[3:4] + head[4:5] + head[5:6]


def kernel(
    n_rows, n_cols, pts_ref, bw_ref, vec_ref, out_ref,
    blk, crs, crs_col, direct, mirror, vec_all, part, t_in, inv,
    fwd_out, fwd_in, rev_out, rev_in,
    zs, zr, ss, sr, cs, cr, ts, tr, fs, fr, gs, gr,
):
    share, width = pts_ref.shape
    k_vec = vec_ref.shape[0]
    f32, bf16 = jnp.float32, jnp.bfloat16
    n = n_cols // 2
    half = HEAD + share // 2
    chunks = [(0, half), (half, share // 2), (HEAD + share, k_vec)]
    row = lax.axis_index("row")
    col = lax.axis_index("col")
    p = col // 2
    core = col % 2
    square = n_rows == 4
    sibling = {"col": p * 2 + 1 - core}

    def row_peer(m):
        return {"row": lax.bitwise_xor(row, m)}

    near_rows = [1, 2] if square else list(range(1, n_rows))
    barrier = pltpu.get_barrier_semaphore()
    pl.semaphore_signal(barrier, inc=1, device_id=sibling, device_id_type=MESH)
    for m in near_rows:
        pl.semaphore_signal(barrier, inc=1, device_id=row_peer(m), device_id_type=MESH)
    has_left = p > 0
    has_right = p < n - 1

    @pl.when(has_left)
    def _():
        pl.semaphore_signal(barrier, inc=1, device_id={"col": col - 2}, device_id_type=MESH)

    @pl.when(has_right)
    def _():
        pl.semaphore_signal(barrier, inc=1, device_id={"col": col + 2}, device_id_type=MESH)

    own = pts_ref[...].astype(f32)
    half_sq = 0.5 * jnp.sum(own * own, axis=1, keepdims=True)
    wide = jnp.transpose(jnp.broadcast_to(half_sq, (share, 128)))
    head = jnp.concatenate(
        [t.astype(f32) for t in terms(bw_ref[...] * (2.0 * LOG2E)) + terms(wide[0:1])]
        + [jnp.zeros((HEAD - 6, share), f32)],
        axis=0,
    ).astype(bf16)
    blk[col, 0:HEAD] = head
    blk[col, HEAD : HEAD + share] = pts_ref[...]
    blk[col, HEAD + share :] = vec_ref[...]
    crs[0, 0:HEAD] = head
    crs[0, HEAD:] = pts_ref[...]
    part[...] = jnp.zeros_like(part)

    beside = has_left.astype(jnp.int32) + has_right.astype(jnp.int32)
    pl.semaphore_wait(barrier, beside + (1 + len(near_rows)))

    def rows(c):
        return pl.ds(chunks[c][0], chunks[c][1])

    def z_copy(side, k, c):
        slot = col + (2 * k if side else -2 * k)
        return pltpu.make_async_remote_copy(
            src_ref=blk.at[slot, rows(c)], dst_ref=blk.at[slot, rows(c)],
            send_sem=zs.at[side, k, c], recv_sem=zr.at[side, k + 1, c],
            device_id={"col": col - 2 if side else col + 2}, device_id_type=MESH,
        )

    def sib_copy(side, k, c, slot):
        return pltpu.make_async_remote_copy(
            src_ref=blk.at[slot, rows(c)], dst_ref=blk.at[slot, rows(c)],
            send_sem=ss.at[side, k, c], recv_sem=sr.at[side, k, c],
            device_id=sibling, device_id_type=MESH,
        )

    def comes(side, k):
        return p + k <= n - 1 if side else p - k >= 0

    def leaves(side, k):
        return comes(side, k) & (has_left if side else has_right)

    def z_send(k, c):
        for side in (0, 1):
            pl.when(leaves(side, k))(lambda: z_copy(side, k, c).start())

    def slot_at(side, k):
        return col + (2 * k if side else -2 * k)

    def z_arrive(k, c):
        for side in (0, 1):

            @pl.when(comes(side, k))
            def _():
                slot = slot_at(side, k)
                pltpu.make_async_remote_copy(
                    src_ref=blk.at[slot, rows(c)], dst_ref=blk.at[slot, rows(c)],
                    send_sem=zs.at[side, k, c], recv_sem=zr.at[side, k, c],
                    device_id=sibling, device_id_type=MESH,
                ).wait_recv()

            if k < n - 1:
                pl.when(leaves(side, k))(lambda: z_copy(side, k, c).start())
            pl.when(comes(side, k))(lambda: sib_copy(side, k, c, slot_at(side, k)).start())

    def sib_arrive(k, cs_):
        other = p * 2 + 1 - core
        for side in (0, 1):
            if k == 0 and side:
                continue

            @pl.when(comes(side, k))
            def _():
                for c in cs_:
                    sib_copy(side, k, c, other + (2 * k if side else -2 * k)).wait_recv()

    def c_copy(src, dst, c, peer):
        source = blk.at[col, rows(c)] if src == 0 else crs.at[src, rows(c)]
        return pltpu.make_async_remote_copy(
            src_ref=source, dst_ref=crs.at[dst, rows(c)],
            send_sem=cs.at[dst, c], recv_sem=cr.at[dst, c], device_id=peer, device_id_type=MESH,
        )

    cross_copies = {}

    def c_send(src, dst, c, peer):
        cross_copies[dst, c] = c_copy(src, dst, c, peer)
        cross_copies[dst, c].start()

    for c in (0, 1):
        z_send(0, c)
        for m in near_rows:
            c_send(0, m, c, row_peer(m))
    for c in (0, 1, 2):
        sib_copy(0, 0, c, col).start()
    z_send(0, 2)

    def column(m):
        spread_row, half_row = untangle(crs[m, 0:HEAD])
        padded = jnp.concatenate([spread_row, half_row, jnp.zeros((6, share), f32)], axis=0)
        crs_col[m] = jnp.transpose(padded)

    def tile(m, slot, diagonal=False):
        cols = crs_col[m]
        arow, hrow = untangle(blk[slot, 0:HEAD])
        cross = lax.dot_general(
            crs[m, HEAD:], blk[slot, HEAD : HEAD + share], NT, preferred_element_type=f32
        )
        near = (cross - cols[:, 1:2]) - hrow
        first = jnp.exp2(near * cols[:, 0:1])
        second = jnp.exp2(near * arow)
        if diagonal:
            same = lax.broadcasted_iota(jnp.int32, (share, share), 0) == lax.broadcasted_iota(
                jnp.int32, (share, share), 1
            )
            first = jnp.where(same, 0.0, first)
            second = jnp.where(same, 0.0, second)
        where = pl.ds(pl.multiple_of(slot * share, share), share)
        direct[m, :, where] = first.astype(bf16)
        mirror[m, :, where] = second.astype(bf16)
        part[slot] += jnp.sum(second, axis=0, keepdims=True)

    def tiles(q, first_m, last_m):
        count = last_m - first_m

        def body(index, carry):
            tile(first_m + index % count, q * 2 + index // count)
            return carry

        if count > 0:
            lax.fori_loop(0, 2 * count, body, 0)

    def nth(s):
        both = jnp.minimum(p, n - 1 - p)
        k_one = s // 2 + 1
        k_two = s - both + 1
        early = p - k_one if s % 2 == 0 else p + k_one
        late = jnp.where(2 * p < n - 1, p + k_two, p - k_two)
        return jnp.where(s < 2 * both, early, late)

    column(0)
    tile(0, col, True)
    sib_arrive(0, (0, 1))
    tile(0, p * 2 + 1 - core)
    for c in (0, 1):
        z_arrive(1, c)
        for m in near_rows:
            cross_copies[m, c].wait_recv()
        if square:
            c_send(*((1, 3, 0, row_peer(2)) if c == 0 else (2, 3, 1, row_peer(1))))
    last = near_rows[-1] + 1
    for m in near_rows:
        column(m)
    tiles(p, 1, last)

    def compute(s, stop):
        sib_arrive(s + 1, (0, 1))
        tiles(nth(s), 0, stop)

    if n > 2:
        z_arrive(2, 0)
        z_arrive(2, 1)
    compute(0, last)
    if square:
        cross_copies[3, 0].wait_recv()
        cross_copies[3, 1].wait_recv()
        column(3)
        tiles(p, 3, 4)
        tiles(nth(0), 3, 4)
    z_arrive(1, 2)
    for s in range(1, n - 1):
        if 3 <= s + 1:
            z_arrive(s + 1, 0)
            z_arrive(s + 1, 1)
        compute(s, n_rows)
        if s + 1 < n - 1:
            z_arrive(s + 1, 2)

    totals = []
    for x in range(1, n_cols):
        copy = pltpu.make_async_remote_copy(
            src_ref=part, dst_ref=t_in.at[x], send_sem=ts.at[x], recv_sem=tr.at[x],
            device_id={"col": lax.bitwise_xor(col, x)}, device_id_type=MESH,
        )
        copy.start()
        totals.append(copy)
    if n > 2:
        z_arrive(n - 1, 2)
    for k in range(n):
        sib_arrive(k, (2,))
    for q in range(n_cols):
        vec_all[:, q * share : (q + 1) * share] = blk[q, HEAD + share :]

    def reduce_send(m, value, out, in_, send, recv):
        out[m] = value.astype(bf16)
        copy = pltpu.make_async_remote_copy(
            src_ref=out.at[m], dst_ref=in_.at[m], send_sem=send.at[m], recv_sem=recv.at[m],
            device_id=row_peer(m), device_id_type=MESH,
        )
        copy.start()
        return copy

    def product(left, right):
        return lax.dot_general(left, right, NT, preferred_element_type=f32)

    order = list(range(n_rows - 1, 0, -1))
    fwd = {m: reduce_send(m, product(vec_all[...], direct[m]), fwd_out, fwd_in, fs, fr) for m in order}
    forward = product(vec_all[...], direct[0])

    total = part[...]
    for x in range(1, n_cols):
        totals[x - 1].wait_recv()
        total = total + t_in[x]
    inverse = 0.125 / total
    inv[...] = inverse
    scaled = jnp.concatenate(
        [
            (vec_all[:, q * share : (q + 1) * share].astype(f32) * inverse[q]).astype(bf16)
            for q in range(n_cols)
        ],
        axis=1,
    )
    rev = {m: reduce_send(m, product(scaled, mirror[m]), rev_out, rev_in, gs, gr) for m in order}
    reverse = product(scaled, mirror[0])
    for m in near_rows + ([3] if square else []):
        fwd[m].wait_recv()
        forward = forward + fwd_in[m].astype(f32)
    forward = forward * inv[col]
    for m in near_rows + ([3] if square else []):
        rev[m].wait_recv()
        reverse = reverse + rev_in[m].astype(f32)
    out_ref[...] = 4.0 * (forward + reverse)

    for group in (cross_copies, fwd, rev):
        for copy in group.values():
            copy.wait_send()
    for copy in totals:
        copy.wait_send()
    for c in (0, 1, 2):
        sib_copy(0, 0, c, col).wait_send()
        for side in (0, 1):
            for k in range(n):
                if k < n - 1:
                    pl.when(leaves(side, k))(lambda: z_copy(side, k, c).wait_send())
                if k > 0:
                    pl.when(comes(side, k))(
                        lambda: sib_copy(side, k, c, slot_at(side, k)).wait_send()
                    )


def local(n_rows, n_cols, points, spread, vectors):
    share, width = points.shape
    k = vectors.shape[1]
    f32, bf16 = jnp.float32, jnp.bfloat16
    dma = pltpu.SemaphoreType.DMA
    n = n_cols // 2
    scratch = [
        pltpu.VMEM((n_cols, HEAD + share + k, width), bf16),
        pltpu.VMEM((n_rows, HEAD + share, width), bf16),
        pltpu.VMEM((n_rows, share, 8), f32),
        pltpu.VMEM((n_rows, share, n_cols * share), bf16),
        pltpu.VMEM((n_rows, share, n_cols * share), bf16),
        pltpu.VMEM((k, n_cols * share), bf16),
        pltpu.VMEM((n_cols, 1, share), f32),
        pltpu.VMEM((n_cols, n_cols, 1, share), f32),
        pltpu.VMEM((n_cols, 1, share), f32),
    ] + [pltpu.VMEM((n_rows, k, share), bf16)] * 4
    scratch += [dma((2, n, 3))] * 4 + [dma((n_rows, 2))] * 2 + [dma((n_cols,))] * 2
    scratch += [dma((n_rows,))] * 4
    out = pl.pallas_call(
        functools.partial(kernel, n_rows, n_cols),
        out_shape=jax.ShapeDtypeStruct((k, share), f32),
        in_specs=[VMEM_SPEC] * 3,
        out_specs=VMEM_SPEC,
        scratch_shapes=scratch,
        compiler_params=pltpu.CompilerParams(
            collective_id=0, has_side_effects=True, vmem_limit_bytes=58 * 1024 * 1024
        ),
    )(points, spread.reshape(1, share), vectors.T)
    return out.T


def solution(mesh):
    placed = (P(("row", "col"), None), P(("row", "col")), P(("row", "col"), None))
    return jax.shard_map(
        functools.partial(local, mesh.shape["row"], mesh.shape["col"]),
        mesh=mesh, in_specs=placed, out_specs=P(("row", "col"), None), check_vma=False,
    )
```

```python
import functools
import math

import jax
import jax.numpy as jnp
from jax import lax
from jax.experimental import pallas as pl
from jax.experimental.pallas import tpu as pltpu
from jax.sharding import PartitionSpec as P

MESH = pl.DeviceIdType.MESH
LOG2E = math.log2(math.e)
VMEM_SPEC = pl.BlockSpec(memory_space=pltpu.VMEM)
HEAD = 16
NT = (((1,), (1,)), ((), ()))


def terms(value):
    high = value.astype(jnp.bfloat16)
    rest = value - high.astype(jnp.float32)
    middle = rest.astype(jnp.bfloat16)
    return [high, middle, (rest - middle.astype(jnp.float32)).astype(jnp.bfloat16)]


def untangle(head):
    head = head.astype(jnp.float32)
    return head[0:1] + head[1:2] + head[2:3], head[3:4] + head[4:5] + head[5:6]


def kernel(
    n_rows, n_cols, pts_ref, bw_ref, vec_ref, out_ref,
    blk, crs, crs_col, direct, mirror, vec_all, part, t_in, inv,
    fwd_out, fwd_in, rev_out, rev_in,
    zs, zr, ss, sr, cs, cr, ts, tr, fs, fr, gs, gr,
):
    share, width = pts_ref.shape
    k_vec = vec_ref.shape[0]
    f32, bf16 = jnp.float32, jnp.bfloat16
    n = n_cols // 2
    half = HEAD + share // 2
    chunks = [(0, half), (half, share // 2), (HEAD + share, k_vec)]
    row = lax.axis_index("row")
    col = lax.axis_index("col")
    p = col // 2
    core = col % 2
    square = n_rows == 4
    sibling = {"col": p * 2 + 1 - core}

    def row_peer(m):
        return {"row": lax.bitwise_xor(row, m)}

    near_rows = [1, 2] if square else list(range(1, n_rows))
    barrier = pltpu.get_barrier_semaphore()
    pl.semaphore_signal(barrier, inc=1, device_id=sibling, device_id_type=MESH)
    for m in near_rows:
        pl.semaphore_signal(barrier, inc=1, device_id=row_peer(m), device_id_type=MESH)
    has_left = p > 0
    has_right = p < n - 1

    @pl.when(has_left)
    def _():
        pl.semaphore_signal(barrier, inc=1, device_id={"col": col - 2}, device_id_type=MESH)

    @pl.when(has_right)
    def _():
        pl.semaphore_signal(barrier, inc=1, device_id={"col": col + 2}, device_id_type=MESH)

    own = pts_ref[...].astype(f32)
    half_sq = 0.5 * jnp.sum(own * own, axis=1, keepdims=True)
    wide = jnp.transpose(jnp.broadcast_to(half_sq, (share, 128)))
    head = jnp.concatenate(
        [t.astype(f32) for t in terms(bw_ref[...] * (2.0 * LOG2E)) + terms(wide[0:1])]
        + [jnp.zeros((HEAD - 6, share), f32)],
        axis=0,
    ).astype(bf16)
    blk[col, 0:HEAD] = head
    blk[col, HEAD : HEAD + share] = pts_ref[...]
    blk[col, HEAD + share :] = vec_ref[...]
    crs[0, 0:HEAD] = head
    crs[0, HEAD:] = pts_ref[...]
    part[...] = jnp.zeros_like(part)

    beside = has_left.astype(jnp.int32) + has_right.astype(jnp.int32)
    pl.semaphore_wait(barrier, beside + (1 + len(near_rows)))

    def rows(c):
        return pl.ds(chunks[c][0], chunks[c][1])

    def z_copy(side, k, c):
        slot = col + (2 * k if side else -2 * k)
        return pltpu.make_async_remote_copy(
            src_ref=blk.at[slot, rows(c)], dst_ref=blk.at[slot, rows(c)],
            send_sem=zs.at[side, k, c], recv_sem=zr.at[side, k + 1, c],
            device_id={"col": col - 2 if side else col + 2}, device_id_type=MESH,
        )

    def sib_copy(side, k, c, slot):
        return pltpu.make_async_remote_copy(
            src_ref=blk.at[slot, rows(c)], dst_ref=blk.at[slot, rows(c)],
            send_sem=ss.at[side, k, c], recv_sem=sr.at[side, k, c],
            device_id=sibling, device_id_type=MESH,
        )

    def comes(side, k):
        return p + k <= n - 1 if side else p - k >= 0

    def leaves(side, k):
        return comes(side, k) & (has_left if side else has_right)

    def z_send(k, c):
        for side in (0, 1):
            pl.when(leaves(side, k))(lambda: z_copy(side, k, c).start())

    def slot_at(side, k):
        return col + (2 * k if side else -2 * k)

    def z_arrive(k, c):
        for side in (0, 1):

            @pl.when(comes(side, k))
            def _():
                slot = slot_at(side, k)
                pltpu.make_async_remote_copy(
                    src_ref=blk.at[slot, rows(c)], dst_ref=blk.at[slot, rows(c)],
                    send_sem=zs.at[side, k, c], recv_sem=zr.at[side, k, c],
                    device_id=sibling, device_id_type=MESH,
                ).wait_recv()

            if k < n - 1:
                pl.when(leaves(side, k))(lambda: z_copy(side, k, c).start())
            pl.when(comes(side, k))(lambda: sib_copy(side, k, c, slot_at(side, k)).start())
            if c == 0:
                pl.when(comes(side, k))(lambda: vec_copy(side, k).start())

    def vec_copy(side, k):
        return pltpu.make_async_remote_copy(
            src_ref=blk.at[col, rows(2)], dst_ref=blk.at[col, rows(2)],
            send_sem=zs.at[side, k, 2], recv_sem=zr.at[1 - side, k, 2],
            device_id={"col": slot_at(side, k)}, device_id_type=MESH,
        )

    def vec_arrive(k):
        for side in (0, 1):

            @pl.when(comes(side, k))
            def _():
                slot = slot_at(side, k)
                pltpu.make_async_remote_copy(
                    src_ref=blk.at[slot, rows(2)], dst_ref=blk.at[slot, rows(2)],
                    send_sem=zs.at[side, k, 2], recv_sem=zr.at[side, k, 2],
                    device_id=sibling, device_id_type=MESH,
                ).wait_recv()
                sib_copy(side, k, 2, slot).start()

    def sib_arrive(k, cs_):
        other = p * 2 + 1 - core
        for side in (0, 1):
            if k == 0 and side:
                continue

            @pl.when(comes(side, k))
            def _():
                for c in cs_:
                    sib_copy(side, k, c, other + (2 * k if side else -2 * k)).wait_recv()

    def c_copy(src, dst, c, peer):
        source = blk.at[col, rows(c)] if src == 0 else crs.at[src, rows(c)]
        return pltpu.make_async_remote_copy(
            src_ref=source, dst_ref=crs.at[dst, rows(c)],
            send_sem=cs.at[dst, c], recv_sem=cr.at[dst, c], device_id=peer, device_id_type=MESH,
        )

    cross_copies = {}

    def c_send(src, dst, c, peer):
        cross_copies[dst, c] = c_copy(src, dst, c, peer)
        cross_copies[dst, c].start()

    for c in (0, 1):
        z_send(0, c)
        for m in near_rows:
            c_send(0, m, c, row_peer(m))
    for c in (0, 1, 2):
        sib_copy(0, 0, c, col).start()

    def column(m):
        spread_row, half_row = untangle(crs[m, 0:HEAD])
        padded = jnp.concatenate([spread_row, half_row, jnp.zeros((6, share), f32)], axis=0)
        crs_col[m] = jnp.transpose(padded)

    def tile(m, slot, diagonal=False):
        cols = crs_col[m]
        arow, hrow = untangle(blk[slot, 0:HEAD])
        cross = lax.dot_general(
            crs[m, HEAD:], blk[slot, HEAD : HEAD + share], NT, preferred_element_type=f32
        )
        near = (cross - cols[:, 1:2]) - hrow
        first = jnp.exp2(near * cols[:, 0:1])
        second = jnp.exp2(near * arow)
        if diagonal:
            same = lax.broadcasted_iota(jnp.int32, (share, share), 0) == lax.broadcasted_iota(
                jnp.int32, (share, share), 1
            )
            first = jnp.where(same, 0.0, first)
            second = jnp.where(same, 0.0, second)
        where = pl.ds(pl.multiple_of(slot * share, share), share)
        direct[m, :, where] = first.astype(bf16)
        mirror[m, :, where] = second.astype(bf16)
        part[slot] += jnp.sum(second, axis=0, keepdims=True)

    def tiles(q, first_m, last_m):
        count = last_m - first_m

        def body(index, carry):
            tile(first_m + index % count, q * 2 + index // count)
            return carry

        if count > 0:
            lax.fori_loop(0, 2 * count, body, 0, unroll=min(2 * count, 8))

    def nth(s):
        both = jnp.minimum(p, n - 1 - p)
        k_one = s // 2 + 1
        k_two = s - both + 1
        early = p - k_one if s % 2 == 0 else p + k_one
        late = jnp.where(2 * p < n - 1, p + k_two, p - k_two)
        return jnp.where(s < 2 * both, early, late)

    column(0)
    tile(0, col, True)
    sib_arrive(0, (0, 1))
    tile(0, p * 2 + 1 - core)
    for c in (0, 1):
        z_arrive(1, c)
        for m in near_rows:
            cross_copies[m, c].wait_recv()
        if square:
            c_send(*((1, 3, 0, row_peer(2)) if c == 0 else (2, 3, 1, row_peer(1))))
    last = near_rows[-1] + 1
    for m in near_rows:
        column(m)
    tiles(p, 1, last)

    def compute(s, stop):
        sib_arrive(s + 1, (0, 1))
        tiles(nth(s), 0, stop)

    if n > 2:
        z_arrive(2, 0)
        z_arrive(2, 1)
    compute(0, last)
    if square:
        cross_copies[3, 0].wait_recv()
        cross_copies[3, 1].wait_recv()
        column(3)
        tiles(p, 3, 4)
        tiles(nth(0), 3, 4)
    for s in range(1, n - 1):
        if s > 1:
            z_arrive(s + 1, 0)
            z_arrive(s + 1, 1)
        compute(s, n_rows)

    totals = []
    for x in range(1, n_cols):
        copy = pltpu.make_async_remote_copy(
            src_ref=part, dst_ref=t_in.at[x], send_sem=ts.at[x], recv_sem=tr.at[x],
            device_id={"col": lax.bitwise_xor(col, x)}, device_id_type=MESH,
        )
        copy.start()
        totals.append(copy)
    for k in range(1, n):
        vec_arrive(k)
    for k in range(n):
        sib_arrive(k, (2,))
    for q in range(n_cols):
        vec_all[:, q * share : (q + 1) * share] = blk[q, HEAD + share :]

    def reduce_send(m, value, out, in_, send, recv):
        out[m] = value.astype(bf16)
        copy = pltpu.make_async_remote_copy(
            src_ref=out.at[m], dst_ref=in_.at[m], send_sem=send.at[m], recv_sem=recv.at[m],
            device_id=row_peer(m), device_id_type=MESH,
        )
        copy.start()
        return copy

    def product(left, right):
        return lax.dot_general(left, right, NT, preferred_element_type=f32)

    order = list(range(n_rows - 1, 0, -1))
    fwd = {m: reduce_send(m, product(vec_all[...], direct[m]), fwd_out, fwd_in, fs, fr) for m in order}
    forward = product(vec_all[...], direct[0])

    total = part[...]
    for x in range(1, n_cols):
        totals[x - 1].wait_recv()
        total = total + t_in[x]
    inverse = 0.125 / total
    inv[...] = inverse
    scaled = jnp.concatenate(
        [
            (vec_all[:, q * share : (q + 1) * share].astype(f32) * inverse[q]).astype(bf16)
            for q in range(n_cols)
        ],
        axis=1,
    )
    rev = {m: reduce_send(m, product(scaled, mirror[m]), rev_out, rev_in, gs, gr) for m in order}
    reverse = product(scaled, mirror[0])
    for m in near_rows + ([3] if square else []):
        fwd[m].wait_recv()
        forward = forward + fwd_in[m].astype(f32)
    forward = forward * inv[col]
    for m in near_rows + ([3] if square else []):
        rev[m].wait_recv()
        reverse = reverse + rev_in[m].astype(f32)
    out_ref[...] = 4.0 * (forward + reverse)

    for group in (cross_copies, fwd, rev):
        for copy in group.values():
            copy.wait_send()
    for copy in totals:
        copy.wait_send()
    for c in (0, 1, 2):
        sib_copy(0, 0, c, col).wait_send()
        for side in (0, 1):
            for k in range(n):
                if c < 2 and k < n - 1:
                    pl.when(leaves(side, k))(lambda: z_copy(side, k, c).wait_send())
                if c == 2 and k > 0:
                    pl.when(comes(side, k))(lambda: vec_copy(side, k).wait_send())
                if k > 0:
                    pl.when(comes(side, k))(
                        lambda: sib_copy(side, k, c, slot_at(side, k)).wait_send()
                    )


def local(n_rows, n_cols, points, spread, vectors):
    share, width = points.shape
    k = vectors.shape[1]
    f32, bf16 = jnp.float32, jnp.bfloat16
    dma = pltpu.SemaphoreType.DMA
    n = n_cols // 2
    scratch = [
        pltpu.VMEM((n_cols, HEAD + share + k, width), bf16),
        pltpu.VMEM((n_rows, HEAD + share, width), bf16),
        pltpu.VMEM((n_rows, share, 8), f32),
        pltpu.VMEM((n_rows, share, n_cols * share), bf16),
        pltpu.VMEM((n_rows, share, n_cols * share), bf16),
        pltpu.VMEM((k, n_cols * share), bf16),
        pltpu.VMEM((n_cols, 1, share), f32),
        pltpu.VMEM((n_cols, n_cols, 1, share), f32),
        pltpu.VMEM((n_cols, 1, share), f32),
    ] + [pltpu.VMEM((n_rows, k, share), bf16)] * 4
    scratch += [dma((2, n, 3))] * 4 + [dma((n_rows, 2))] * 2 + [dma((n_cols,))] * 2
    scratch += [dma((n_rows,))] * 4
    out = pl.pallas_call(
        functools.partial(kernel, n_rows, n_cols),
        out_shape=jax.ShapeDtypeStruct((k, share), f32),
        in_specs=[VMEM_SPEC] * 3,
        out_specs=VMEM_SPEC,
        scratch_shapes=scratch,
        compiler_params=pltpu.CompilerParams(
            collective_id=0, has_side_effects=True, vmem_limit_bytes=58 * 1024 * 1024
        ),
    )(points, spread.reshape(1, share), vectors.T)
    return out.T


def solution(mesh):
    placed = (P(("row", "col"), None), P(("row", "col")), P(("row", "col"), None))
    return jax.shard_map(
        functools.partial(local, mesh.shape["row"], mesh.shape["col"]),
        mesh=mesh, in_specs=placed, out_specs=P(("row", "col"), None), check_vma=False,
    )
```

```python
import functools
import math

import jax
import jax.numpy as jnp
from jax import lax
from jax.experimental import pallas as pl
from jax.experimental.pallas import tpu as pltpu
from jax.sharding import PartitionSpec as P

MESH = pl.DeviceIdType.MESH
LOG2E = math.log2(math.e)
VMEM_SPEC = pl.BlockSpec(memory_space=pltpu.VMEM)
ANY_SPEC = pl.BlockSpec(memory_space=pl.ANY)
PIECES = 2
HEAD = 16
NT = (((1,), (1,)), ((), ()))


def terms(value):
    high = value.astype(jnp.bfloat16)
    rest = value - high.astype(jnp.float32)
    middle = rest.astype(jnp.bfloat16)
    return [high, middle, (rest - middle.astype(jnp.float32)).astype(jnp.bfloat16)]


def untangle(head):
    head = head.astype(jnp.float32)
    return head[0:1] + head[1:2] + head[2:3], head[3:4] + head[4:5] + head[5:6]


def kernel(
    n_rows, n_cols, pts_ref, bw_ref, vec_ref, out_ref,
    blk, crs, crs_col, direct, mirror, vec_all, part, t_in, inv,
    fwd_out, fwd_in, rev_out, rev_in,
    zs, zr, ss, sr, cs, cr, ts, tr, fs, fr, gs, gr, ls,
):
    share, width = pts_ref.shape
    k_vec = vec_ref.shape[0]
    f32, bf16 = jnp.float32, jnp.bfloat16
    n = n_cols // 2
    half = HEAD + share // 2
    halves = [(0, half), (half, share // 2)]
    piece = share // PIECES
    chunks = [(0, HEAD + piece)] + [(HEAD + c * piece, piece) for c in range(1, PIECES)]
    chunks.append((HEAD + share, k_vec))
    points, vecs = tuple(range(PIECES)), PIECES
    row = lax.axis_index("row")
    col = lax.axis_index("col")
    p = col // 2
    core = col % 2
    square = n_rows == 4
    sibling = {"col": p * 2 + 1 - core}

    def row_peer(m):
        return {"row": lax.bitwise_xor(row, m)}

    near_rows = [1, 2] if square else list(range(1, n_rows))
    barrier = pltpu.get_barrier_semaphore()
    pl.semaphore_signal(barrier, inc=1, device_id=sibling, device_id_type=MESH)
    for m in near_rows:
        pl.semaphore_signal(barrier, inc=1, device_id=row_peer(m), device_id_type=MESH)
    has_left = p > 0
    has_right = p < n - 1

    @pl.when(has_left)
    def _():
        pl.semaphore_signal(barrier, inc=1, device_id={"col": col - 2}, device_id_type=MESH)

    @pl.when(has_right)
    def _():
        pl.semaphore_signal(barrier, inc=1, device_id={"col": col + 2}, device_id_type=MESH)

    loads = [
        pltpu.make_async_copy(pts_ref, crs.at[0, pl.ds(HEAD, share)], ls.at[0]),
        pltpu.make_async_copy(pts_ref, blk.at[col, pl.ds(HEAD, share)], ls.at[1]),
        pltpu.make_async_copy(vec_ref, blk.at[col, pl.ds(HEAD + share, k_vec)], ls.at[2]),
    ]
    for load in loads:
        load.start()
    loads[0].wait()
    own = crs[0, HEAD:].astype(f32)
    half_sq = 0.5 * jnp.sum(own * own, axis=1, keepdims=True)
    wide = jnp.transpose(jnp.broadcast_to(half_sq, (share, 128)))
    head = jnp.concatenate(
        [t.astype(f32) for t in terms(bw_ref[...] * (2.0 * LOG2E)) + terms(wide[0:1])]
        + [jnp.zeros((HEAD - 6, share), f32)],
        axis=0,
    ).astype(bf16)
    blk[col, 0:HEAD] = head
    crs[0, 0:HEAD] = head
    part[...] = jnp.zeros_like(part)
    loads[1].wait()
    loads[2].wait()

    beside = has_left.astype(jnp.int32) + has_right.astype(jnp.int32)
    pl.semaphore_wait(barrier, beside + (1 + len(near_rows)))

    def rows(c):
        return pl.ds(chunks[c][0], chunks[c][1])

    def z_copy(side, k, c):
        slot = col + (2 * k if side else -2 * k)
        return pltpu.make_async_remote_copy(
            src_ref=blk.at[slot, rows(c)], dst_ref=blk.at[slot, rows(c)],
            send_sem=zs.at[side, k, c], recv_sem=zr.at[side, k + 1, c],
            device_id={"col": col - 2 if side else col + 2}, device_id_type=MESH,
        )

    def sib_copy(side, k, c, slot):
        return pltpu.make_async_remote_copy(
            src_ref=blk.at[slot, rows(c)], dst_ref=blk.at[slot, rows(c)],
            send_sem=ss.at[side, k, c], recv_sem=sr.at[side, k, c],
            device_id=sibling, device_id_type=MESH,
        )

    def comes(side, k):
        return p + k <= n - 1 if side else p - k >= 0

    def leaves(side, k):
        return comes(side, k) & (has_left if side else has_right)

    def z_send(k, c):
        for side in (0, 1):
            pl.when(leaves(side, k))(lambda: z_copy(side, k, c).start())

    def slot_at(side, k):
        return col + (2 * k if side else -2 * k)

    def z_arrive(k, c):
        for side in (0, 1):

            @pl.when(comes(side, k))
            def _():
                slot = slot_at(side, k)
                pltpu.make_async_remote_copy(
                    src_ref=blk.at[slot, rows(c)], dst_ref=blk.at[slot, rows(c)],
                    send_sem=zs.at[side, k, c], recv_sem=zr.at[side, k, c],
                    device_id=sibling, device_id_type=MESH,
                ).wait_recv()

            if k < n - 1:
                pl.when(leaves(side, k))(lambda: z_copy(side, k, c).start())
            pl.when(comes(side, k))(lambda: sib_copy(side, k, c, slot_at(side, k)).start())
            if c == 0 and k > 2:
                pl.when(comes(side, k))(lambda: vec_copy(side, k).start())

    def vec_copy(side, k):
        return pltpu.make_async_remote_copy(
            src_ref=blk.at[col, rows(vecs)], dst_ref=blk.at[col, rows(vecs)],
            send_sem=zs.at[side, k, vecs], recv_sem=zr.at[1 - side, k, vecs],
            device_id={"col": slot_at(side, k)}, device_id_type=MESH,
        )

    def vec_arrive(k):
        for side in (0, 1):

            @pl.when(comes(side, k))
            def _():
                slot = slot_at(side, k)
                pltpu.make_async_remote_copy(
                    src_ref=blk.at[slot, rows(vecs)], dst_ref=blk.at[slot, rows(vecs)],
                    send_sem=zs.at[side, k, vecs], recv_sem=zr.at[side, k, vecs],
                    device_id=sibling, device_id_type=MESH,
                ).wait_recv()
                sib_copy(side, k, vecs, slot).start()

    def sib_arrive(k, cs_):
        other = p * 2 + 1 - core
        for side in (0, 1):
            if k == 0 and side:
                continue

            @pl.when(comes(side, k))
            def _():
                for c in cs_:
                    sib_copy(side, k, c, other + (2 * k if side else -2 * k)).wait_recv()

    def c_copy(src, dst, c, peer):
        part_rows = pl.ds(*halves[c])
        source = blk.at[col, part_rows] if src == 0 else crs.at[src, part_rows]
        return pltpu.make_async_remote_copy(
            src_ref=source, dst_ref=crs.at[dst, part_rows],
            send_sem=cs.at[dst, c], recv_sem=cr.at[dst, c], device_id=peer, device_id_type=MESH,
        )

    cross_copies = {}

    def c_send(src, dst, c, peer):
        cross_copies[dst, c] = c_copy(src, dst, c, peer)
        cross_copies[dst, c].start()

    for c in points:
        z_send(0, c)
    for c in (0, 1):
        for m in near_rows:
            c_send(0, m, c, row_peer(m))
    for c in range(PIECES + 1):
        sib_copy(0, 0, c, col).start()

    def column(m):
        spread_row, half_row = untangle(crs[m, 0:HEAD])
        padded = jnp.concatenate([spread_row, half_row, jnp.zeros((6, share), f32)], axis=0)
        crs_col[m] = jnp.transpose(padded)

    def tile(m, slot, diagonal=False):
        cols = crs_col[m]
        arow, hrow = untangle(blk[slot, 0:HEAD])
        cross = lax.dot_general(
            crs[m, HEAD:], blk[slot, HEAD : HEAD + share], NT, preferred_element_type=f32
        )
        near = (cross - cols[:, 1:2]) - hrow
        first = jnp.exp2(near * cols[:, 0:1])
        second = jnp.exp2(near * arow)
        if diagonal:
            same = lax.broadcasted_iota(jnp.int32, (share, share), 0) == lax.broadcasted_iota(
                jnp.int32, (share, share), 1
            )
            first = jnp.where(same, 0.0, first)
            second = jnp.where(same, 0.0, second)
        where = pl.ds(pl.multiple_of(slot * share, share), share)
        direct[m, :, where] = first.astype(bf16)
        mirror[m, :, where] = second.astype(bf16)
        part[slot] += jnp.sum(second, axis=0, keepdims=True)

    def tiles(q, first_m, last_m):
        count = last_m - first_m

        def body(index, carry):
            tile(first_m + index % count, q * 2 + index // count)
            return carry

        if count > 0:
            lax.fori_loop(0, 2 * count, body, 0, unroll=min(2 * count, 8))

    def nth(s):
        both = jnp.minimum(p, n - 1 - p)
        k_one = s // 2 + 1
        k_two = s - both + 1
        early = p - k_one if s % 2 == 0 else p + k_one
        late = jnp.where(2 * p < n - 1, p + k_two, p - k_two)
        return jnp.where(s < 2 * both, early, late)

    column(0)
    tile(0, col, True)
    sib_arrive(0, points)
    tile(0, p * 2 + 1 - core)
    for c in points:
        z_arrive(1, c)
    for c in (0, 1):
        for m in near_rows:
            cross_copies[m, c].wait_recv()
        if square:
            c_send(*((1, 3, 0, row_peer(2)) if c == 0 else (2, 3, 1, row_peer(1))))
    last = near_rows[-1] + 1
    for m in near_rows:
        column(m)
    tiles(p, 1, last)

    def compute(s, stop):
        sib_arrive(s + 1, points)
        tiles(nth(s), 0, stop)

    if n > 2:
        for c in points:
            z_arrive(2, c)
    for k in range(1, min(n, 3)):
        for side in (0, 1):
            pl.when(comes(side, k))(lambda: vec_copy(side, k).start())
    compute(0, last)
    if square:
        cross_copies[3, 0].wait_recv()
        cross_copies[3, 1].wait_recv()
        column(3)
        tiles(p, 3, 4)
        tiles(nth(0), 3, 4)
    for s in range(1, n - 1):
        if s > 1:
            for c in points:
                z_arrive(s + 1, c)
        compute(s, n_rows)

    totals = []
    for x in range(1, n_cols):
        copy = pltpu.make_async_remote_copy(
            src_ref=part, dst_ref=t_in.at[x], send_sem=ts.at[x], recv_sem=tr.at[x],
            device_id={"col": lax.bitwise_xor(col, x)}, device_id_type=MESH,
        )
        copy.start()
        totals.append(copy)
    for k in range(1, n):
        vec_arrive(k)
    for k in range(n):
        sib_arrive(k, (vecs,))
    for q in range(n_cols):
        vec_all[:, q * share : (q + 1) * share] = blk[q, HEAD + share :]

    def reduce_send(m, value, out, in_, send, recv):
        out[m] = value.astype(bf16)
        copy = pltpu.make_async_remote_copy(
            src_ref=out.at[m], dst_ref=in_.at[m], send_sem=send.at[m], recv_sem=recv.at[m],
            device_id=row_peer(m), device_id_type=MESH,
        )
        copy.start()
        return copy

    def product(left, right):
        return lax.dot_general(left, right, NT, preferred_element_type=f32)

    order = list(range(n_rows - 1, 0, -1))
    fwd = {m: reduce_send(m, product(vec_all[...], direct[m]), fwd_out, fwd_in, fs, fr) for m in order}
    forward = product(vec_all[...], direct[0])

    total = part[...]
    for x in range(1, n_cols):
        totals[x - 1].wait_recv()
        total = total + t_in[x]
    inverse = 0.125 / total
    inv[...] = inverse
    scaled = jnp.concatenate(
        [
            (vec_all[:, q * share : (q + 1) * share].astype(f32) * inverse[q]).astype(bf16)
            for q in range(n_cols)
        ],
        axis=1,
    )
    rev = {m: reduce_send(m, product(scaled, mirror[m]), rev_out, rev_in, gs, gr) for m in order}
    reverse = product(scaled, mirror[0])
    for m in near_rows + ([3] if square else []):
        fwd[m].wait_recv()
        forward = forward + fwd_in[m].astype(f32)
    forward = forward * inv[col]
    for m in near_rows + ([3] if square else []):
        rev[m].wait_recv()
        reverse = reverse + rev_in[m].astype(f32)
    out_ref[...] = 4.0 * (forward + reverse)

    for group in (cross_copies, fwd, rev):
        for copy in group.values():
            copy.wait_send()
    for copy in totals:
        copy.wait_send()
    for c in range(PIECES + 1):
        sib_copy(0, 0, c, col).wait_send()
        for side in (0, 1):
            for k in range(n):
                if c < vecs and k < n - 1:
                    pl.when(leaves(side, k))(lambda: z_copy(side, k, c).wait_send())
                if c == vecs and k > 0:
                    pl.when(comes(side, k))(lambda: vec_copy(side, k).wait_send())
                if k > 0:
                    pl.when(comes(side, k))(
                        lambda: sib_copy(side, k, c, slot_at(side, k)).wait_send()
                    )


def local(n_rows, n_cols, points, spread, vectors):
    share, width = points.shape
    k = vectors.shape[1]
    f32, bf16 = jnp.float32, jnp.bfloat16
    dma = pltpu.SemaphoreType.DMA
    n = n_cols // 2
    scratch = [
        pltpu.VMEM((n_cols, HEAD + share + k, width), bf16),
        pltpu.VMEM((n_rows, HEAD + share, width), bf16),
        pltpu.VMEM((n_rows, share, 8), f32),
        pltpu.VMEM((n_rows, share, n_cols * share), bf16),
        pltpu.VMEM((n_rows, share, n_cols * share), bf16),
        pltpu.VMEM((k, n_cols * share), bf16),
        pltpu.VMEM((n_cols, 1, share), f32),
        pltpu.VMEM((n_cols, n_cols, 1, share), f32),
        pltpu.VMEM((n_cols, 1, share), f32),
    ] + [pltpu.VMEM((n_rows, k, share), bf16)] * 4
    scratch += [dma((2, n, PIECES + 1))] * 4 + [dma((n_rows, 2))] * 2 + [dma((n_cols,))] * 2
    scratch += [dma((n_rows,))] * 4 + [dma((3,))]
    out = pl.pallas_call(
        functools.partial(kernel, n_rows, n_cols),
        out_shape=jax.ShapeDtypeStruct((k, share), f32),
        in_specs=[ANY_SPEC, VMEM_SPEC, ANY_SPEC],
        out_specs=VMEM_SPEC,
        scratch_shapes=scratch,
        compiler_params=pltpu.CompilerParams(
            collective_id=0, has_side_effects=True, vmem_limit_bytes=58 * 1024 * 1024
        ),
    )(points, spread.reshape(1, share), vectors.T)
    return out.T


def solution(mesh):
    placed = (P(("row", "col"), None), P(("row", "col")), P(("row", "col"), None))
    return jax.shard_map(
        functools.partial(local, mesh.shape["row"], mesh.shape["col"]),
        mesh=mesh, in_specs=placed, out_specs=P(("row", "col"), None), check_vma=False,
    )
```
